32 devices in a mesh: pipe: 8 (over y, x, core), tensor: 4 (over z).
Axes of the slice: x: 2, y: 2, z: 4, core: 2. Of those that a mesh axis runs over, the one named last changes fastest.
Arguments:
- down_state: bfloat16 [8, 128, 4096], P('pipe', None, 'tensor'), may hold values from -64 to 64
- up_state: bfloat16 [8, 128, 4096], P('pipe', None, 'tensor'), may hold values from -64 to 64
- layer_proj: bfloat16 [8, 4096, 4096], P('pipe', 'tensor'), may hold values from -0.125 to 0.125
- conv_filters: float32 [8, 256, 128], P('pipe', 'tensor'), may hold values from -1.5 to 1.5
- norm_gains: float32 [8, 4096], P('pipe', 'tensor'), may hold values from 0.5 to 1.5
- embedding: bfloat16 [512, 4096], P(None, 'tensor'), may hold values from -6 to 6
- dna_tokens: int32 [2, 8, 128], replicated, may hold values from 0 to 511
- entry_order: int32 [2, 8], replicated, may hold values from 0 to 7, each once within a row
Outputs:
- section_outputs: bfloat16 [3, 2, 8, 128, 4096], P(None, None, 'pipe', None, 'tensor')
The draws below stay inside these ranges and needn't reach their ends.
All inputs are finite; a program needn't handle non-finite values.
Results may differ from the reference program's by a relative error of at most 0.0065.
Values may be sent and summed in bfloat16 or wider, within the bound.
No kernel may reach another device: no remote copies, remote signals or barrier semaphores. Data moves between devices by JAX's collectives and lax.ppermute only.
A program may use at most 64 MiB of HBM per device.

```python
import math
import jax
import jax.numpy as jnp
import numpy as np
from jax import lax

WIDTH = 4096
GROUP_SIZE = 16
SHORT_TAPS = 7
LONG_TAPS = 128
VOCAB_SIZE = 512
SEQ_LEN = 128
TICK_COUNT = 3
WAITING = 8
SECTIONS = 8
N_TENSOR = 4


def state_draw(key):
    keys = jax.random.split(key, 3)
    shape = (SECTIONS, SEQ_LEN, WIDTH)
    column = jnp.arange(WIDTH).astype(jnp.float32) / WIDTH
    column_scale = 3.0 ** column * jnp.exp(jax.random.uniform(keys[1], (WIDTH,), jnp.float32) * jnp.log(3.0))
    row_scale = jnp.exp(jax.random.uniform(keys[2], (SECTIONS, SEQ_LEN, 1), jnp.float32) * jnp.log(10.0))
    base = jnp.clip(jax.random.normal(keys[0], shape, jnp.float32), -3.5, 3.5)
    values = jnp.clip(base * column_scale * row_scale, -64.0, 64.0)
    return values.astype(jnp.bfloat16)


def draw_down_state(key, part):
    return state_draw(jax.random.fold_in(key, 11))


def draw_up_state(key, part):
    return state_draw(jax.random.fold_in(key, 23))


def with_ends(values, stream_key, smallest, top_value):
    dims = values.shape
    spot = [jax.random.randint(jax.random.fold_in(stream_key, axis), (), 0, dims[axis]) for axis in range(len(dims))]
    values = values.at[tuple(spot)].set(smallest)
    longest = dims.index(max(dims))
    spot[longest] = (spot[longest] + 1) % dims[longest]
    return values.at[tuple(spot)].set(top_value)


def raised(entries, key, source, target, shards_of, factor):
    owner, partner = [(jnp.arange(entries.shape[dim]) // (entries.shape[dim] // shards_of)).reshape([-1 if axis == dim else 1 for axis in range(entries.ndim)]) for dim in (source, target)]
    chosen = jax.random.permutation(key, shards_of)[partner]
    strong = (owner == chosen) | (owner == (partner + shards_of // 2) % shards_of)
    return jnp.where(strong, factor * entries, entries)


def level_of(rng, dims, cuts, least, largest):
    factor_of = 1.0
    for position, parts in cuts:
        heights = jax.random.uniform(jax.random.fold_in(jax.random.fold_in(rng, 6), position), (parts,), jnp.float32, least / len(cuts), largest / len(cuts))
        factor_of = factor_of * jnp.repeat(jnp.exp(heights), dims[position] // parts).reshape((-1,) + (1,) * (len(dims) - 1 - position))
    return factor_of


def rank_bounds(number_of, lean):
    loads = [(1 << 20) // math.isqrt(rank ** lean) + 1 for rank in range(1, number_of + 1)]
    deviation = 1 + sum(loads) // (1 << 30)
    return np.cumsum(np.array([max(1, weight // deviation) for weight in loads]))


def skewed_ids(key, dims, count, slope):
    grid = rank_bounds(count, slope)
    pick = jax.random.randint(jax.random.fold_in(key, 1), dims, 0, int(grid[count - 1]))
    standing = jnp.searchsorted(jnp.asarray(grid, jnp.int32), pick, side="right")
    return jax.random.permutation(jax.random.fold_in(key, 2), count)[standing].astype(jnp.int32)


def gaussian(stream_key, shape, spread, most, shards=(), held_as=jnp.bfloat16):
    entries = spread * jax.random.normal(stream_key, shape, jnp.float32)
    if shards:
        entries = entries * level_of(stream_key, shape, shards, -0.22, 0.18)
    return jnp.clip(entries, -most, most).astype(held_as)


def heavy_noise(rng, dims, scale, limit, shards, heavy, dtype=jnp.bfloat16):
    drawn = scale * jax.random.normal(rng, dims, jnp.float32)
    if shards:
        drawn = drawn * level_of(rng, dims, shards, -0.22, 0.18)
    return jnp.clip(raised(drawn, jax.random.fold_in(rng, 3), *heavy), -limit, limit).astype(dtype)


def setup_inputs(seed: int = 0) -> dict:
    splits = jax.random.split(jax.random.key(seed), 9)
    down_state = draw_down_state(jax.random.fold_in(splits[8], 71), 0)
    up_state = draw_up_state(jax.random.fold_in(splits[8], 71), 0)
    layer_proj = heavy_noise(splits[2], (SECTIONS, WIDTH, WIDTH), WIDTH ** -0.5, 0.125, ((0, 8), (1, 4)), (1, 2, 4, 2.0))
    conv_filters = gaussian(splits[3], (SECTIONS, WIDTH // GROUP_SIZE, LONG_TAPS), 0.25, 1.5, ((0, 8), (1, 4)), jnp.float32)
    norm_gains = jnp.clip(1.0 + 0.1 * jax.random.normal(splits[4], (SECTIONS, WIDTH), jnp.float32), 0.5, 1.5)
    embedding = gaussian(splits[5], (VOCAB_SIZE, WIDTH), 1.0, 6.0, ((1, 4),))
    dna_tokens = with_ends(skewed_ids(splits[6], (2, WAITING, SEQ_LEN), VOCAB_SIZE, 2), jax.random.fold_in(splits[6], 3), 0, VOCAB_SIZE - 1).astype(jnp.int32)
    entry_order = jax.vmap(lambda own: jax.random.permutation(own, WAITING))(jax.random.split(splits[7], 2)).reshape((2, WAITING)).astype(jnp.int32)
    return {"down_state": down_state, "up_state": up_state, "layer_proj": layer_proj, "conv_filters": conv_filters, "norm_gains": norm_gains, "embedding": embedding, "dna_tokens": dna_tokens, "entry_order": entry_order}


EPSILON = 1e-06

def causal_mixing(normed, filters, taps):
    seq = normed.shape[0]
    groups = filters.shape[0]
    longest = filters.shape[1]
    later = lax.broadcasted_iota(jnp.int32, (seq, seq), 0)
    earlier = lax.broadcasted_iota(jnp.int32, (seq, seq), 1)
    offsets = (later - earlier).astype(jnp.int32)
    picked = filters[:, jnp.clip(offsets, 0, longest - 1)]
    toeplitz = jnp.where((offsets >= 0) & (offsets < taps), picked, jnp.zeros_like(picked))
    grouped = normed.reshape(seq, groups, -1)
    mixed = jnp.einsum('gts,sgc->tgc', toeplitz, grouped, precision=lax.Precision.HIGHEST)
    return mixed.reshape(seq, -1)

def layer_step(inputs):
    layer_input, weight, filters, gains, taps = inputs
    values = layer_input.astype(jnp.float32)
    squares = lax.optimization_barrier(jnp.sum(values * values, axis=-1))
    normed = values * lax.rsqrt(squares / WIDTH + EPSILON)[..., None] * gains
    mixed = jax.vmap(lambda piece: causal_mixing(piece, filters, taps))(normed)
    gated = (normed * mixed).astype(jnp.bfloat16).reshape(-1, WIDTH)
    blocked = gated.astype(jnp.float32).reshape(-1, N_TENSOR, WIDTH // N_TENSOR)
    wblock = weight.astype(jnp.float32).reshape(N_TENSOR, WIDTH // N_TENSOR, WIDTH)
    partial_value = jnp.einsum('rtk,tkn->rtn', blocked, wblock).astype(jnp.bfloat16)
    partial_value = lax.optimization_barrier(partial_value)
    summed = lax.optimization_barrier(jnp.sum(partial_value.astype(jnp.float32), axis=1))
    result = (values.reshape(-1, WIDTH) + summed).astype(jnp.bfloat16)
    return result.reshape(layer_input.shape)

def reference(down_state, up_state, layer_proj, conv_filters, norm_gains, embedding, dna_tokens, entry_order):
    section_ids = jnp.arange(SECTIONS).astype(jnp.int32)
    taps_all = jnp.where(section_ids % 2 == 0, SHORT_TAPS, LONG_TAPS).astype(jnp.int32)
    downward = down_state
    upward = up_state[::-1]
    records = []
    for tick in range(TICK_COUNT):
        if tick > 0:
            fresh_down = embedding[dna_tokens[0, entry_order[0, tick - 1]]]
            fresh_up = embedding[dna_tokens[1, entry_order[1, tick - 1]]]
            downward = jnp.concatenate([fresh_down[None], downward[:-1]], axis=0)
            upward = jnp.concatenate([fresh_up[None], upward[:-1]], axis=0)
        paired = jnp.stack([downward, upward], axis=1)
        result = lax.map(layer_step, (paired, layer_proj, conv_filters, norm_gains, taps_all))
        downward = result[:, 0]
        upward = result[:, 1]
        records.append(jnp.stack([downward, upward[::-1]], axis=0))
    return jnp.stack(records)
```

```python
import functools

import jax
import jax.numpy as jnp
from jax import lax
from jax.experimental import pallas as pl
from jax.experimental.pallas import tpu as pltpu
from jax.sharding import PartitionSpec as P

WIDTH = 4096
SHORT_TAPS = 7
LONG_TAPS = 128
GROUP_SIZE = 16
TICK_COUNT = 3
EPSILON = 1e-06

LANES = 128
PER_BLOCK = LANES // GROUP_SIZE
IN_VMEM = pl.BlockSpec(memory_space=pltpu.VMEM)
IN_SMEM = pl.BlockSpec(memory_space=pltpu.SMEM)
IN_PLACE = pl.BlockSpec(memory_space=pl.ANY)


def toeplitz_kernel(taps_ref, filters_ref, blocks_ref):
    groups, seq = filters_ref.shape
    lane = lax.broadcasted_iota(jnp.int32, (groups, seq), 1)
    kept = jnp.where(lane < taps_ref[0], filters_ref[...], 0.0).astype(jnp.bfloat16)
    row = lax.broadcasted_iota(jnp.int32, (seq, seq), 0)
    col = lax.broadcasted_iota(jnp.int32, (seq, seq), 1)
    flip = ((row + col) % seq == 0).astype(jnp.bfloat16)
    backward = jnp.dot(kept, flip, preferred_element_type=jnp.float32)
    for group in range(groups):
        wide = jnp.broadcast_to(backward[group : group + 1, :], (seq, seq))
        turned = pltpu.roll(wide, 0, 1, stride=1, stride_axis=0)
        start = group % PER_BLOCK * seq
        blocks_ref[group // PER_BLOCK, :, start : start + seq] = jnp.where(
            row >= col, turned, 0.0
        ).astype(jnp.bfloat16)


def toeplitz_blocks(filters, taps):
    groups, seq = filters.shape
    return pl.pallas_call(
        toeplitz_kernel,
        out_shape=jax.ShapeDtypeStruct((groups // PER_BLOCK, seq, PER_BLOCK * seq), jnp.bfloat16),
        in_specs=[IN_SMEM, IN_VMEM],
        out_specs=IN_VMEM,
        name="toeplitz",
    )(taps, filters)


def row_squares(values):
    seq, channels = values.shape
    squares = values * values
    total = squares[:, :LANES]
    for start in range(LANES, channels, LANES):
        total = total + squares[:, start : start + LANES]
    return jnp.sum(total.T, axis=0, keepdims=True)


def squares_kernel(values_ref, squares_ref):
    squares_ref[...] = row_squares(values_ref[...].astype(jnp.float32))


def squares_of(values):
    return pl.pallas_call(
        squares_kernel,
        out_shape=jax.ShapeDtypeStruct((1, values.shape[0]), jnp.float32),
        in_specs=[IN_VMEM],
        out_specs=IN_VMEM,
        name="squares",
    )(values)


def layer_kernel(count, place_ref, x_ref, gains_ref, blocks_ref, weight_ref, *refs):
    squares_refs, refs = refs[: count - 1], refs[count - 1 :]
    out_refs, (weight_buf, gated_buf, sems) = refs[:count], refs[count:]
    place = place_ref[0]
    seq, channels = x_ref.shape
    order = [apart for apart in reversed(range(count))]
    copies = {}
    for apart in order:
        start = pl.multiple_of((place ^ apart) * channels, channels)
        copies[apart] = pltpu.make_async_copy(
            weight_ref.at[:, pl.ds(start, channels)], weight_buf.at[apart], sems.at[apart]
        )
        copies[apart].start()
    values = x_ref[...].astype(jnp.float32)
    others = squares_refs[0][...]
    for ref in squares_refs[1:]:
        others = others + ref[...]
    squares = jnp.broadcast_to(others, (seq, seq)).T + jnp.sum(
        values * values, axis=-1, keepdims=True
    )
    scale = lax.rsqrt(squares / WIDTH + EPSILON)
    lane_group = lax.broadcasted_iota(jnp.int32, (seq, LANES), 1) // GROUP_SIZE
    for block in range(channels // LANES):
        lanes = slice(block * LANES, (block + 1) * LANES)
        normed = values[:, lanes] * scale * gains_ref[:, lanes]
        narrow = normed.astype(jnp.bfloat16)
        spread = jnp.concatenate(
            [
                jnp.where(lane_group == part, narrow, jnp.zeros_like(narrow))
                for part in range(PER_BLOCK)
            ],
            axis=0,
        )
        mixed = jnp.dot(blocks_ref[block], spread, preferred_element_type=jnp.float32)
        gated_buf[:, lanes] = (normed * mixed).astype(jnp.bfloat16)
    for apart in order:
        copies[apart].wait()
        out_refs[apart][...] = jnp.dot(
            gated_buf[...], weight_buf[apart], preferred_element_type=jnp.float32
        ).astype(out_refs[apart].dtype)


def layer_partials(x, squares, place, gains, blocks, weight, count):
    seq, channels = x.shape
    kinds = [jnp.bfloat16 if apart % 2 else jnp.float32 for apart in range(count)]
    return pl.pallas_call(
        functools.partial(layer_kernel, count),
        out_shape=[jax.ShapeDtypeStruct((seq, channels), kind) for kind in kinds],
        in_specs=[IN_SMEM, IN_VMEM, IN_VMEM, IN_VMEM, IN_PLACE] + [IN_VMEM] * (count - 1),
        out_specs=[IN_VMEM] * count,
        scratch_shapes=[
            pltpu.VMEM((count, channels, channels), jnp.bfloat16),
            pltpu.VMEM((seq, channels), jnp.bfloat16),
            pltpu.SemaphoreType.DMA((count,)),
        ],
        compiler_params=pltpu.CompilerParams(vmem_limit_bytes=40 * 2**20),
        name="layer",
    )(place, x, gains, blocks, weight, *squares)


def merge_kernel(count, last_ref, x_ref, fresh_ref, own_ref, *refs):
    arrived, (y_ref, sent_ref, squares_ref) = refs[:count], refs[count:]
    total = own_ref[...]
    for ref in arrived:
        total = total + ref[...].astype(jnp.float32)
    y = (x_ref[...].astype(jnp.float32) + total).astype(jnp.bfloat16)
    y_ref[...] = y
    sent = jnp.where(last_ref[0] == 1, fresh_ref[...].astype(jnp.float32), y.astype(jnp.float32))
    sent_ref[...] = sent.astype(jnp.bfloat16)
    squares_ref[...] = row_squares(sent)


def merge(x, fresh, own, arrived, last):
    seq, channels = x.shape
    return pl.pallas_call(
        functools.partial(merge_kernel, len(arrived)),
        out_shape=[
            jax.ShapeDtypeStruct((seq, channels), jnp.bfloat16),
            jax.ShapeDtypeStruct((seq, channels), jnp.bfloat16),
            jax.ShapeDtypeStruct((1, seq), jnp.float32),
        ],
        in_specs=[IN_SMEM] + [IN_VMEM] * (3 + len(arrived)),
        out_specs=[IN_VMEM] * 3,
        name="merge",
    )(last, x, fresh, own, *arrived)


def embed_tokens(token_ids, table):
    onehot = (
        token_ids[:, None]
        == lax.broadcasted_iota(jnp.int32, (token_ids.shape[0], table.shape[0]), 1)
    ).astype(jnp.bfloat16)
    return jnp.dot(onehot, table, preferred_element_type=jnp.float32).astype(jnp.bfloat16)


def send(values, target):
    pipe, tensor = lax.axis_size("pipe"), lax.axis_size("tensor")
    pairs = []
    for k in range(pipe):
        for z in range(tensor):
            to_k, to_z = target(k, z)
            pairs.append((k * tensor + z, to_k * tensor + to_z))
    return lax.ppermute(values, ("pipe", "tensor"), pairs)


def add_up(partials):
    count = len(partials)
    partials = list(partials)
    arrived = []
    bit = 1
    while bit < count:
        for apart in reversed(range(bit, count, 2 * bit)):
            outgoing = partials[apart].astype(jnp.bfloat16)
            incoming = send(outgoing, lambda k, z: (k, z ^ bit))
            if apart == bit:
                arrived.append(incoming)
            else:
                partials[apart ^ bit] = partials[apart ^ bit] + incoming.astype(jnp.float32)
        bit *= 2
    return arrived


def local(
    down_state, up_state, layer_proj, conv_filters, norm_gains, embedding, dna_tokens, entry_order
):
    pipe, tensor = lax.axis_size("pipe"), lax.axis_size("tensor")
    section = lax.axis_index("pipe")
    place = lax.axis_index("tensor").astype(jnp.int32).reshape(1)
    last = (section == pipe - 1).astype(jnp.int32).reshape(1)
    taps = jnp.where(section % 2 == 0, SHORT_TAPS, LONG_TAPS).astype(jnp.int32).reshape(1)
    weight, gains = layer_proj[0], norm_gains

    def mirrored(k):
        return pipe - 1 - k

    def following(k):
        return (k + 1) % pipe

    def spread_squares(squares, target):
        return [
            send(squares, lambda k, z, apart=apart: (target(k), z ^ apart))
            for apart in range(1, tensor)
        ]

    entering = [down_state[0], up_state[0]]
    squares = [squares_of(values) for values in entering]
    squares = [spread_squares(squares[0], lambda k: k), spread_squares(squares[1], mirrored)]
    entering[1] = send(entering[1], lambda k, z: (mirrored(k), z))
    blocks = toeplitz_blocks(conv_filters[0], taps)
    fresh = [
        [
            embed_tokens(dna_tokens[way, entry_order[way, tick]], embedding)
            for tick in range(TICK_COUNT - 1)
        ]
        for way in range(2)
    ]
    records = []
    for tick in range(TICK_COUNT):
        leaving = []
        for way in range(2):
            x = entering[way]
            partials = layer_partials(x, squares[way], place, gains, blocks, weight, tensor)
            arrived = add_up(partials)
            newcomer = fresh[way][min(tick, TICK_COUNT - 2)]
            y, sent, own = merge(x, newcomer, partials[0], arrived, last)
            if tick < TICK_COUNT - 1:
                squares[way] = spread_squares(own, following)
                entering[way] = send(sent, lambda k, z: (following(k), z))
            leaving.append(y if way == 0 else send(y, lambda k, z: (mirrored(k), z)))
        records.append(jnp.stack(leaving))
    return jnp.stack(records)[:, :, None]


def solution(mesh):
    placed = (
        P("pipe", None, "tensor"),
        P("pipe", None, "tensor"),
        P("pipe", "tensor", None),
        P("pipe", "tensor", None),
        P("pipe", "tensor"),
        P(None, "tensor"),
        P(),
        P(),
    )
    return jax.shard_map(
        local,
        mesh=mesh,
        in_specs=placed,
        out_specs=P(None, None, "pipe", None, "tensor"),
        check_vma=False,
    )
```

```python
import functools

import jax
import jax.numpy as jnp
from jax import lax
from jax.experimental import pallas as pl
from jax.experimental.pallas import tpu as pltpu
from jax.sharding import PartitionSpec as P

WIDTH = 4096
SHORT_TAPS = 7
LONG_TAPS = 128
GROUP_SIZE = 16
TICK_COUNT = 3
EPSILON = 1e-06

LANES = 128
PER_BLOCK = LANES // GROUP_SIZE
IN_VMEM = pl.BlockSpec(memory_space=pltpu.VMEM)
IN_SMEM = pl.BlockSpec(memory_space=pltpu.SMEM)
IN_PLACE = pl.BlockSpec(memory_space=pl.ANY)
IN_HBM = pl.BlockSpec(memory_space=pltpu.HBM)


def toeplitz_kernel(taps_ref, filters_ref, blocks_ref):
    groups, seq = filters_ref.shape
    lane = lax.broadcasted_iota(jnp.int32, (groups, seq), 1)
    kept = jnp.where(lane < taps_ref[0], filters_ref[...], 0.0).astype(jnp.bfloat16)
    row = lax.broadcasted_iota(jnp.int32, (seq, seq), 0)
    col = lax.broadcasted_iota(jnp.int32, (seq, seq), 1)
    flip = ((row + col) % seq == 0).astype(jnp.bfloat16)
    backward = jnp.dot(kept, flip, preferred_element_type=jnp.float32)
    for group in range(groups):
        wide = jnp.broadcast_to(backward[group : group + 1, :], (seq, seq))
        turned = pltpu.roll(wide, 0, 1, stride=1, stride_axis=0)
        start = group % PER_BLOCK * seq
        blocks_ref[group // PER_BLOCK, :, start : start + seq] = jnp.where(
            row >= col, turned, 0.0
        ).astype(jnp.bfloat16)


def toeplitz_blocks(filters, taps):
    groups, seq = filters.shape
    return pl.pallas_call(
        toeplitz_kernel,
        out_shape=jax.ShapeDtypeStruct((groups // PER_BLOCK, seq, PER_BLOCK * seq), jnp.bfloat16),
        in_specs=[IN_SMEM, IN_VMEM],
        out_specs=IN_VMEM,
        compiler_params=pltpu.CompilerParams(vmem_limit_bytes=6 * 2**20),
        name="toeplitz",
    )(taps, filters)


def row_squares(values):
    seq, channels = values.shape
    squares = values * values
    total = squares[:, :LANES]
    for start in range(LANES, channels, LANES):
        total = total + squares[:, start : start + LANES]
    return jnp.sum(total.T, axis=0, keepdims=True)


def squares_kernel(count, *refs):
    for values_ref, squares_ref in zip(refs[:count], refs[count:]):
        squares_ref[...] = row_squares(values_ref[...].astype(jnp.float32))


def squares_of(*arrays):
    return pl.pallas_call(
        functools.partial(squares_kernel, len(arrays)),
        out_shape=[jax.ShapeDtypeStruct((1, array.shape[0]), jnp.float32) for array in arrays],
        in_specs=[IN_VMEM] * len(arrays),
        out_specs=[IN_VMEM] * len(arrays),
        compiler_params=pltpu.CompilerParams(vmem_limit_bytes=6 * 2**20),
        name="squares",
    )(*arrays)


def layer_kernel(count, place_ref, x_ref, gains_ref, blocks_ref, weight_ref, *refs):
    squares_refs, refs = refs[: count - 1], refs[count - 1 :]
    refs = refs[-count - 3 :]
    out_refs, (weight_buf, gated_buf, sems) = refs[:count], refs[count:]
    place = place_ref[0]
    seq, channels = x_ref.shape
    order = [apart for apart in reversed(range(count))]
    copies = {}
    for apart in order:
        start = pl.multiple_of((place ^ apart) * channels, channels)
        copies[apart] = pltpu.make_async_copy(
            weight_ref.at[:, pl.ds(start, channels)], weight_buf.at[apart], sems.at[apart]
        )
        copies[apart].start()
    values = x_ref[...].astype(jnp.float32)
    others = squares_refs[0][...]
    for ref in squares_refs[1:]:
        others = others + ref[...]
    squares = jnp.broadcast_to(others, (seq, seq)).T + jnp.sum(
        values * values, axis=-1, keepdims=True
    )
    scale = lax.rsqrt(squares / WIDTH + EPSILON)
    lane_group = lax.broadcasted_iota(jnp.int32, (seq, LANES), 1) // GROUP_SIZE
    for block in range(channels // LANES):
        lanes = slice(block * LANES, (block + 1) * LANES)
        normed = values[:, lanes] * scale * gains_ref[:, lanes]
        narrow = normed.astype(jnp.bfloat16)
        spread = jnp.concatenate(
            [
                jnp.where(lane_group == part, narrow, jnp.zeros_like(narrow))
                for part in range(PER_BLOCK)
            ],
            axis=0,
        )
        mixed = jnp.dot(blocks_ref[block], spread, preferred_element_type=jnp.float32)
        gated_buf[:, lanes] = (normed * mixed).astype(jnp.bfloat16)
    for apart in order:
        copies[apart].wait()
        out_refs[apart][...] = jnp.dot(
            gated_buf[...], weight_buf[apart], preferred_element_type=jnp.float32
        ).astype(out_refs[apart].dtype)


def layer_partials(x, squares, place, gains, blocks, weight, count, after):
    seq, channels = x.shape
    kinds = [jnp.bfloat16 if apart % 2 else jnp.float32 for apart in range(count)]
    return pl.pallas_call(
        functools.partial(layer_kernel, count),
        out_shape=[jax.ShapeDtypeStruct((seq, channels), kind) for kind in kinds],
        in_specs=[IN_SMEM, IN_VMEM, IN_VMEM, IN_VMEM, IN_HBM]
        + [IN_VMEM] * (count - 1)
        + [IN_PLACE] * len(after),
        out_specs=[IN_VMEM] * count,
        scratch_shapes=[
            pltpu.VMEM((count, channels, channels), jnp.bfloat16),
            pltpu.VMEM((seq, channels), jnp.bfloat16),
            pltpu.SemaphoreType.DMA((count,)),
        ],
        compiler_params=pltpu.CompilerParams(vmem_limit_bytes=20 * 2**20),
        cost_estimate=pl.CostEstimate(
            flops=2 * seq * channels * (channels * count + PER_BLOCK * seq),
            transcendentals=0,
            bytes_accessed=2 * channels * channels * count,
        ),
        name="layer",
    )(place, x, gains, blocks, weight, *squares, *after)


def merge_kernel(count, last_ref, x_ref, fresh_ref, own_ref, *refs):
    arrived, (y_ref, sent_ref, squares_ref) = refs[:count], refs[count:]
    total = own_ref[...]
    for ref in arrived:
        total = total + ref[...].astype(jnp.float32)
    y = (x_ref[...].astype(jnp.float32) + total).astype(jnp.bfloat16)
    y_ref[...] = y
    sent = jnp.where(last_ref[0] == 1, fresh_ref[...].astype(jnp.float32), y.astype(jnp.float32))
    sent_ref[...] = sent.astype(jnp.bfloat16)
    squares_ref[...] = row_squares(sent)


def merge(x, fresh, own, arrived, last):
    seq, channels = x.shape
    return pl.pallas_call(
        functools.partial(merge_kernel, len(arrived)),
        out_shape=[
            jax.ShapeDtypeStruct((seq, channels), jnp.bfloat16),
            jax.ShapeDtypeStruct((seq, channels), jnp.bfloat16),
            jax.ShapeDtypeStruct((1, seq), jnp.float32),
        ],
        in_specs=[IN_SMEM] + [IN_VMEM] * (3 + len(arrived)),
        out_specs=[IN_VMEM] * 3,
        compiler_params=pltpu.CompilerParams(vmem_limit_bytes=6 * 2**20),
        name="merge",
    )(last, x, fresh, own, *arrived)


def embed_tokens(token_ids, table):
    onehot = (
        token_ids[:, None]
        == lax.broadcasted_iota(jnp.int32, (token_ids.shape[0], table.shape[0]), 1)
    ).astype(jnp.bfloat16)
    return jnp.dot(onehot, table, preferred_element_type=jnp.float32).astype(jnp.bfloat16)


def send(values, target):
    pipe, tensor = lax.axis_size("pipe"), lax.axis_size("tensor")
    pairs = []
    for k in range(pipe):
        for z in range(tensor):
            to_k, to_z = target(k, z)
            pairs.append((k * tensor + z, to_k * tensor + to_z))
    return lax.ppermute(values, ("pipe", "tensor"), pairs)


def add_up(partials):
    count = len(partials)
    partials = list(partials)
    arrived, early = [], None
    bit = 1
    while bit < count:
        for apart in reversed(range(bit, count, 2 * bit)):
            outgoing = partials[apart].astype(jnp.bfloat16)
            if apart == bit and bit < count // 2:
                ahead = partials[2 * bit].astype(jnp.bfloat16)
                early = ahead if early is None else early
                outgoing, partials[2 * bit] = lax.optimization_barrier((outgoing, ahead))
            incoming = send(outgoing, lambda k, z: (k, z ^ bit))
            if apart == bit:
                arrived.append(incoming)
            else:
                partials[apart ^ bit] = partials[apart ^ bit].astype(
                    jnp.float32
                ) + incoming.astype(jnp.float32)
        bit *= 2
    return arrived, early


def local(
    down_state, up_state, layer_proj, conv_filters, norm_gains, embedding, dna_tokens, entry_order
):
    pipe, tensor = lax.axis_size("pipe"), lax.axis_size("tensor")
    section = lax.axis_index("pipe")
    place = lax.axis_index("tensor").astype(jnp.int32).reshape(1)
    last = (section == pipe - 1).astype(jnp.int32).reshape(1)
    taps = jnp.where(section % 2 == 0, SHORT_TAPS, LONG_TAPS).astype(jnp.int32).reshape(1)
    weight, gains = layer_proj[0], norm_gains

    def mirrored(k):
        return pipe - 1 - k

    def following(k):
        return (k + 1) % pipe

    def spread_squares(squares, target):
        return [
            send(squares, lambda k, z, apart=apart: (target(k), z ^ apart))
            for apart in range(1, tensor)
        ]

    entering = [down_state[0], up_state[0]]
    squares = squares_of(*entering)
    entering[1] = send(entering[1], lambda k, z: (mirrored(k), z))
    squares = [spread_squares(squares[0], lambda k: k), spread_squares(squares[1], mirrored)]
    blocks = toeplitz_blocks(conv_filters[0], taps)
    fresh = [
        [
            embed_tokens(dna_tokens[way, entry_order[way, tick]], embedding)
            for tick in range(TICK_COUNT - 1)
        ]
        for way in range(2)
    ]
    leaving = [[], []]
    after = []
    for tick in range(TICK_COUNT):
        for way in (1, 0):
            x = entering[way]
            partials = layer_partials(
                x, squares[way], place, gains, blocks, weight, tensor, after
            )
            arrived, early = add_up(partials)
            after = [] if early is None else [early]
            newcomer = fresh[way][min(tick, TICK_COUNT - 2)]
            y, sent, own = merge(x, newcomer, partials[0], arrived, last)
            if tick < TICK_COUNT - 1:
                squares[way] = spread_squares(own, following)
                entering[way] = send(sent, lambda k, z: (following(k), z))
            leaving[way].append(send(y, lambda k, z: (mirrored(k), z)) if way else y)
    return jnp.stack([jnp.stack(way) for way in leaving], axis=1)[:, :, None]


def solution(mesh):
    placed = (
        P("pipe", None, "tensor"),
        P("pipe", None, "tensor"),
        P("pipe", "tensor", None),
        P("pipe", "tensor", None),
        P("pipe", "tensor"),
        P(None, "tensor"),
        P(),
        P(),
    )
    return jax.shard_map(
        local,
        mesh=mesh,
        in_specs=placed,
        out_specs=P(None, None, "pipe", None, "tensor"),
        check_vma=False,
    )
```

```python
import functools

import jax
import jax.numpy as jnp
from jax import lax
from jax.experimental import pallas as pl
from jax.experimental.pallas import tpu as pltpu
from jax.sharding import PartitionSpec as P

WIDTH = 4096
SHORT_TAPS = 7
LONG_TAPS = 128
GROUP_SIZE = 16
TICK_COUNT = 3
EPSILON = 1e-06

LANES = 128
PER_BLOCK = LANES // GROUP_SIZE
IN_VMEM = pl.BlockSpec(memory_space=pltpu.VMEM)
IN_PLACE = pl.BlockSpec(memory_space=pl.ANY)


def prepare_kernel(
    ticks, order_hbm, filters_hbm, tokens_hbm, table_hbm, weight_hbm, *refs
):
    blocks_ref, weight_ref, refs = refs[0], refs[1], refs[2:]
    fresh_refs, refs = refs[: 2 * ticks], refs[2 * ticks :]
    order_ref, filters_ref, tokens_ref, table_ref, sems = refs
    copies = [
        pltpu.make_async_copy(source, target, sems.at[spot])
        for spot, (source, target) in enumerate(
            [
                (filters_hbm, filters_ref),
                (order_hbm, order_ref),
                (tokens_hbm, tokens_ref),
                (table_hbm, table_ref),
                (weight_hbm, weight_ref),
            ]
        )
    ]
    for copy in copies:
        copy.start()
    copies[0].wait()
    groups, seq = filters_ref.shape
    taps = jnp.where(lax.axis_index("pipe") % 2 == 0, SHORT_TAPS, LONG_TAPS)
    lane = lax.broadcasted_iota(jnp.int32, (groups, seq), 1)
    kept = jnp.where(lane < taps, filters_ref[...], 0.0).astype(jnp.bfloat16)
    row = lax.broadcasted_iota(jnp.int32, (seq, seq), 0)
    col = lax.broadcasted_iota(jnp.int32, (seq, seq), 1)
    flip = ((row + col) % seq == 0).astype(jnp.bfloat16)
    backward = jnp.dot(kept, flip, preferred_element_type=jnp.float32)
    for group in range(groups):
        wide = jnp.broadcast_to(backward[group : group + 1, :], (seq, seq))
        turned = pltpu.roll(wide, 0, 1, stride=1, stride_axis=0)
        start = group % PER_BLOCK * seq
        blocks_ref[group // PER_BLOCK, :, start : start + seq] = jnp.where(
            row >= col, turned, 0.0
        ).astype(jnp.bfloat16)
    for copy in copies[1:4]:
        copy.wait()
    word = lax.broadcasted_iota(jnp.int32, (table_ref.shape[0], seq), 0)
    for entry, fresh_ref in enumerate(fresh_refs):
        way, tick = entry // ticks, entry % ticks
        chosen = tokens_ref[way, pl.ds(order_ref[way, tick], 1), :]
        onehot = (word == chosen).astype(jnp.bfloat16)
        fresh_ref[...] = lax.dot_general(
            onehot, table_ref[...], (((0,), (0,)), ((), ())), preferred_element_type=jnp.float32
        ).astype(fresh_ref.dtype)
    copies[4].wait()


def in_hbm(array):
    return pltpu.with_memory_space_constraint(array, pltpu.HBM)


def prepare(filters, weight, tokens, order, table):
    groups, seq = filters.shape
    ticks = TICK_COUNT - 1
    blocks, held, *fresh = pl.pallas_call(
        functools.partial(prepare_kernel, ticks),
        out_shape=[
            jax.ShapeDtypeStruct((groups // PER_BLOCK, seq, PER_BLOCK * seq), jnp.bfloat16),
            jax.ShapeDtypeStruct(weight.shape, weight.dtype),
        ]
        + [jax.ShapeDtypeStruct((seq, table.shape[1]), table.dtype)] * (2 * ticks),
        in_specs=[IN_PLACE] * 5,
        out_specs=[IN_VMEM] * (2 + 2 * ticks),
        scratch_shapes=[
            pltpu.SMEM(order.shape, order.dtype),
            pltpu.VMEM(filters.shape, filters.dtype),
            pltpu.VMEM(tokens.shape, tokens.dtype),
            pltpu.VMEM(table.shape, table.dtype),
            pltpu.SemaphoreType.DMA((5,)),
        ],
        compiler_params=pltpu.CompilerParams(vmem_limit_bytes=16 * 2**20),
        name="prepare",
    )(in_hbm(order), in_hbm(filters), in_hbm(tokens), in_hbm(table), in_hbm(weight))
    return blocks, held, [fresh[:ticks], fresh[ticks:]]


def row_squares(values):
    seq, channels = values.shape
    squares = values * values
    total = squares[:, :LANES]
    for start in range(LANES, channels, LANES):
        total = total + squares[:, start : start + LANES]
    return jnp.sum(total.T, axis=0, keepdims=True)


def squares_kernel(count, *refs):
    sources, squares_ref, held_ref, sems = refs[:count], refs[-3], refs[-2], refs[-1]
    copies = [
        pltpu.make_async_copy(source, held_ref.at[spot], sems.at[spot])
        for spot, source in enumerate(sources)
    ]
    for copy in copies:
        copy.start()
    for spot, copy in enumerate(copies):
        copy.wait()
        squares_ref[spot : spot + 1, :] = row_squares(held_ref[spot].astype(jnp.float32))


def squares_of(*arrays):
    count = len(arrays)
    return pl.pallas_call(
        functools.partial(squares_kernel, count),
        out_shape=jax.ShapeDtypeStruct((count, arrays[0].shape[0]), jnp.float32),
        in_specs=[IN_PLACE] * count,
        out_specs=IN_VMEM,
        scratch_shapes=[
            pltpu.VMEM((count, *arrays[0].shape), arrays[0].dtype),
            pltpu.SemaphoreType.DMA((count,)),
        ],
        compiler_params=pltpu.CompilerParams(vmem_limit_bytes=6 * 2**20),
        name="squares",
    )(*[in_hbm(array) for array in arrays])


def layer_kernel(count, line, x_ref, gains_ref, blocks_ref, weight_ref, *refs):
    squares_refs, out_refs, gated_buf = refs[: count - 1], refs[-count - 1 : -1], refs[-1]
    place = lax.axis_index("tensor")
    seq, channels = x_ref.shape
    values = x_ref[...].astype(jnp.float32)
    others = squares_refs[0][line : line + 1, :]
    for ref in squares_refs[1:]:
        others = others + ref[line : line + 1, :]
    squares = jnp.broadcast_to(others, (seq, seq)).T + jnp.sum(
        values * values, axis=-1, keepdims=True
    )
    scale = lax.rsqrt(squares / WIDTH + EPSILON)
    lane_group = lax.broadcasted_iota(jnp.int32, (seq, LANES), 1) // GROUP_SIZE
    for block in range(channels // LANES):
        lanes = slice(block * LANES, (block + 1) * LANES)
        normed = values[:, lanes] * scale * gains_ref[:, lanes]
        narrow = normed.astype(jnp.bfloat16)
        spread = jnp.concatenate(
            [
                jnp.where(lane_group == part, narrow, jnp.zeros_like(narrow))
                for part in range(PER_BLOCK)
            ],
            axis=0,
        )
        mixed = jnp.dot(blocks_ref[block], spread, preferred_element_type=jnp.float32)
        gated_buf[:, lanes] = (normed * mixed).astype(jnp.bfloat16)
    for apart in reversed(range(count)):
        start = pl.multiple_of((place ^ apart) * channels, channels)
        out_refs[apart][...] = jnp.dot(
            gated_buf[...],
            weight_ref[:, pl.ds(start, channels)],
            preferred_element_type=jnp.float32,
        ).astype(out_refs[apart].dtype)


def layer_partials(x, squares, line, gains, blocks, weight, count, after):
    seq, channels = x.shape
    kinds = [jnp.bfloat16 if apart % 2 else jnp.float32 for apart in range(count)]
    return pl.pallas_call(
        functools.partial(layer_kernel, count, line),
        out_shape=[jax.ShapeDtypeStruct((seq, channels), kind) for kind in kinds],
        in_specs=[IN_VMEM] * (3 + count) + [IN_PLACE] * len(after),
        out_specs=[IN_VMEM] * count,
        scratch_shapes=[pltpu.VMEM((seq, channels), jnp.bfloat16)],
        compiler_params=pltpu.CompilerParams(vmem_limit_bytes=12 * 2**20),
        cost_estimate=pl.CostEstimate(
            flops=1 * 2 * seq * channels * channels * count,
            transcendentals=0,
            bytes_accessed=1 * 2 * channels * channels * count,
        ),
        name="layer",
    )(x, gains, blocks, weight, *squares, *after)


def merge_kernel(count, x_ref, fresh_ref, own_ref, *refs):
    arrived, (y_ref, sent_ref, squares_ref) = refs[:count], refs[-3:]
    total = own_ref[...]
    for ref in arrived:
        total = total + ref[...].astype(jnp.float32)
    y = (x_ref[...].astype(jnp.float32) + total).astype(jnp.bfloat16)
    y_ref[...] = y
    last = lax.axis_index("pipe") == lax.axis_size("pipe") - 1
    sent = jnp.where(last, fresh_ref[...].astype(jnp.float32), y.astype(jnp.float32))
    sent_ref[...] = sent.astype(jnp.bfloat16)
    squares_ref[...] = row_squares(sent)


def merge(x, fresh, own, arrived, after):
    seq, channels = x.shape
    return pl.pallas_call(
        functools.partial(merge_kernel, len(arrived)),
        out_shape=[
            jax.ShapeDtypeStruct((seq, channels), jnp.bfloat16),
            jax.ShapeDtypeStruct((seq, channels), jnp.bfloat16),
            jax.ShapeDtypeStruct((1, seq), jnp.float32),
        ],
        in_specs=[IN_VMEM] * (3 + len(arrived)) + [IN_PLACE] * len(after),
        out_specs=[IN_VMEM] * 3,
        compiler_params=pltpu.CompilerParams(vmem_limit_bytes=6 * 2**20),
        name="merge",
    )(x, fresh, own, *arrived, *after)


def send(values, target):
    pipe, tensor = lax.axis_size("pipe"), lax.axis_size("tensor")
    pairs = []
    for k in range(pipe):
        for z in range(tensor):
            to_k, to_z = target(k, z)
            pairs.append((k * tensor + z, to_k * tensor + to_z))
    return lax.ppermute(values, ("pipe", "tensor"), pairs)


def first_halving(partials, after):
    partials = list(partials)
    for apart in reversed(range(3, len(partials), 2)):
        incoming = send(partials[apart], lambda k, z: (k, z ^ 1))
        incoming, after = lax.optimization_barrier((incoming, after))
        partials[apart ^ 1] = partials[apart ^ 1] + incoming.astype(jnp.float32)
    kept = partials[:2] + [
        partial.astype(jnp.bfloat16) if apart == 2 else partial
        for apart, partial in enumerate(partials)
        if apart >= 2 and apart % 2 == 0
    ]
    return kept, after


def other_halvings(partials):
    pair, rest = partials[:2], partials[2:]
    arrived = [send(pair[1], lambda k, z: (k, z ^ 1))]
    left = {2 * (spot + 1): partial for spot, partial in enumerate(rest)}
    bit = 2
    while left:
        for apart in sorted(left, reverse=True):
            if apart & bit:
                incoming = send(
                    left.pop(apart).astype(jnp.bfloat16), lambda k, z: (k, z ^ bit)
                )
                if apart == bit:
                    arrived.append(incoming)
                else:
                    left[apart ^ bit] = left[apart ^ bit].astype(jnp.float32) + incoming.astype(
                        jnp.float32
                    )
        bit *= 2
    return arrived


def local(
    down_state, up_state, layer_proj, conv_filters, norm_gains, embedding, dna_tokens, entry_order
):
    pipe, tensor = lax.axis_size("pipe"), lax.axis_size("tensor")
    gains = norm_gains

    def mirrored(k):
        return pipe - 1 - k

    def following(k):
        return (k + 1) % pipe

    def spread(sums, target):
        return [
            send(sums, lambda k, z, apart=apart: (target(k), z ^ apart))
            for apart in range(1, tensor)
        ]

    down, up = 0, 1
    entering = [down_state[0], up_state[0]]
    sums = squares_of(*entering)
    squares = [spread(sums, lambda k: k), spread(sums, mirrored)]
    entering[up] = send(entering[up], lambda k, z: (mirrored(k), z))
    blocks, weight, fresh = prepare(
        conv_filters[0], layer_proj[0], dna_tokens, entry_order, embedding
    )

    def go_on(partials):
        own, *rest = partials
        rest = lax.optimization_barrier(rest)
        return own, other_halvings([own, *rest]), rest[1:2]

    def run_layer(way, tick, after, held):
        *partials, neighbour = layer_partials(
            entering[way],
            squares[way],
            way if tick == 0 else 0,
            gains,
            blocks,
            weight,
            tensor,
            after,
        )
        if way == up and tick > 0:
            neighbour, y = lax.optimization_barrier((neighbour, leaving[up].pop()))
            leaving[up].append(send(y, lambda k, z: (mirrored(k), z)))
        return first_halving([*partials, neighbour], held)

    def finish(way, tick, own, arrived):
        newcomer = fresh[way][min(tick, TICK_COUNT - 2)]
        y, sent, sums = merge(entering[way], newcomer, own, arrived, leaving[way][-1:])
        leaving[way].append(y)
        if tick < TICK_COUNT - 1:
            entering[way] = send(sent, lambda k, z: (following(k), z))
            squares[way] = spread(sums, following)

    leaving = [[], []]
    early = []
    for tick in range(TICK_COUNT):
        for way in (up, down):
            ending = tick == TICK_COUNT - 1 and way == down
            held = [leaving[up].pop()] if ending else []
            partials, held = run_layer(way, tick, early, held)
            leaving[up].extend(held)
            own, arrived, early = go_on(partials)
            finish(way, tick, own, arrived)
    leaving[up].append(send(leaving[up].pop(), lambda k, z: (mirrored(k), z)))
    return jnp.stack([jnp.stack(way) for way in leaving], axis=1)[:, :, None]


def solution(mesh):
    placed = (
        P("pipe", None, "tensor"),
        P("pipe", None, "tensor"),
        P("pipe", "tensor", None),
        P("pipe", "tensor", None),
        P("pipe", "tensor"),
        P(None, "tensor"),
        P(),
        P(),
    )
    return jax.shard_map(
        local,
        mesh=mesh,
        in_specs=placed,
        out_specs=P(None, None, "pipe", None, "tensor"),
        check_vma=False,
    )
```

```python
import functools

import jax
import jax.numpy as jnp
from jax import lax
from jax.experimental import pallas as pl
from jax.experimental.pallas import tpu as pltpu
from jax.sharding import PartitionSpec as P

WIDTH = 4096
SHORT_TAPS = 7
LONG_TAPS = 128
GROUP_SIZE = 16
TICK_COUNT = 3
EPSILON = 1e-06

LANES = 128
PER_BLOCK = LANES // GROUP_SIZE
IN_VMEM = pl.BlockSpec(memory_space=pltpu.VMEM)
IN_PLACE = pl.BlockSpec(memory_space=pl.ANY)


def prepare_kernel(
    ticks, order_hbm, filters_hbm, tokens_hbm, table_hbm, weight_hbm, *refs
):
    blocks_ref, weight_ref, refs = refs[0], refs[1], refs[2:]
    fresh_refs, refs = refs[: 2 * ticks], refs[2 * ticks :]
    order_ref, filters_ref, tokens_ref, table_ref, sems = refs
    copies = [
        pltpu.make_async_copy(source, target, sems.at[spot])
        for spot, (source, target) in enumerate(
            [
                (filters_hbm, filters_ref),
                (order_hbm, order_ref),
                (tokens_hbm, tokens_ref),
                (table_hbm, table_ref),
                (weight_hbm, weight_ref),
            ]
        )
    ]
    for copy in copies:
        copy.start()
    copies[0].wait()
    groups, seq = filters_ref.shape
    taps = jnp.where(lax.axis_index("pipe") % 2 == 0, SHORT_TAPS, LONG_TAPS)
    lane = lax.broadcasted_iota(jnp.int32, (groups, seq), 1)
    kept = jnp.where(lane < taps, filters_ref[...], 0.0).astype(jnp.bfloat16)
    row = lax.broadcasted_iota(jnp.int32, (seq, seq), 0)
    col = lax.broadcasted_iota(jnp.int32, (seq, seq), 1)
    flip = ((row + col) % seq == 0).astype(jnp.bfloat16)
    backward = jnp.dot(kept, flip, preferred_element_type=jnp.float32)
    for group in range(groups):
        wide = jnp.broadcast_to(backward[group : group + 1, :], (seq, seq))
        turned = pltpu.roll(wide, 0, 1, stride=1, stride_axis=0)
        start = group % PER_BLOCK * seq
        blocks_ref[group // PER_BLOCK, :, start : start + seq] = jnp.where(
            row >= col, turned, 0.0
        ).astype(jnp.bfloat16)
    for copy in copies[1:4]:
        copy.wait()
    word = lax.broadcasted_iota(jnp.int32, (table_ref.shape[0], seq), 0)
    for entry, fresh_ref in enumerate(fresh_refs):
        way, tick = entry // ticks, entry % ticks
        chosen = tokens_ref[way, pl.ds(order_ref[way, tick], 1), :]
        onehot = (word == chosen).astype(jnp.bfloat16)
        fresh_ref[...] = lax.dot_general(
            onehot, table_ref[...], (((0,), (0,)), ((), ())), preferred_element_type=jnp.float32
        ).astype(fresh_ref.dtype)
    copies[4].wait()


def in_hbm(array):
    return pltpu.with_memory_space_constraint(array, pltpu.HBM)


def prepare(filters, weight, tokens, order, table):
    groups, seq = filters.shape
    ticks = TICK_COUNT - 1
    blocks, held, *fresh = pl.pallas_call(
        functools.partial(prepare_kernel, ticks),
        out_shape=[
            jax.ShapeDtypeStruct((groups // PER_BLOCK, seq, PER_BLOCK * seq), jnp.bfloat16),
            jax.ShapeDtypeStruct(weight.shape, weight.dtype),
        ]
        + [jax.ShapeDtypeStruct((seq, table.shape[1]), table.dtype)] * (2 * ticks),
        in_specs=[IN_PLACE] * 5,
        out_specs=[IN_VMEM] * (2 + 2 * ticks),
        scratch_shapes=[
            pltpu.SMEM(order.shape, order.dtype),
            pltpu.VMEM(filters.shape, filters.dtype),
            pltpu.VMEM(tokens.shape, tokens.dtype),
            pltpu.VMEM(table.shape, table.dtype),
            pltpu.SemaphoreType.DMA((5,)),
        ],
        compiler_params=pltpu.CompilerParams(vmem_limit_bytes=16 * 2**20),
        name="prepare",
    )(in_hbm(order), in_hbm(filters), in_hbm(tokens), in_hbm(table), in_hbm(weight))
    return blocks, held, [fresh[:ticks], fresh[ticks:]]


def row_squares(values):
    seq, channels = values.shape
    squares = values * values
    total = squares[:, :LANES]
    for start in range(LANES, channels, LANES):
        total = total + squares[:, start : start + LANES]
    return jnp.sum(total.T, axis=0, keepdims=True)


def squares_kernel(count, *refs):
    sources, squares_ref, held_ref, sems = refs[:count], refs[-3], refs[-2], refs[-1]
    copies = [
        pltpu.make_async_copy(source, held_ref.at[spot], sems.at[spot])
        for spot, source in enumerate(sources)
    ]
    for copy in copies:
        copy.start()
    for spot, copy in enumerate(copies):
        copy.wait()
        squares_ref[spot : spot + 1, :] = row_squares(held_ref[spot].astype(jnp.float32))


def squares_of(*arrays):
    count = len(arrays)
    return pl.pallas_call(
        functools.partial(squares_kernel, count),
        out_shape=jax.ShapeDtypeStruct((count, arrays[0].shape[0]), jnp.float32),
        in_specs=[IN_PLACE] * count,
        out_specs=IN_VMEM,
        scratch_shapes=[
            pltpu.VMEM((count, *arrays[0].shape), arrays[0].dtype),
            pltpu.SemaphoreType.DMA((count,)),
        ],
        compiler_params=pltpu.CompilerParams(vmem_limit_bytes=6 * 2**20),
        name="squares",
    )(*[in_hbm(array) for array in arrays])


def layer_kernel(count, line, x_ref, gains_ref, blocks_ref, weight_ref, *refs):
    squares_refs, out_refs, gated_buf = refs[: count - 1], refs[-count - 1 : -1], refs[-1]
    place = lax.axis_index("tensor")
    seq, channels = x_ref.shape
    values = x_ref[...].astype(jnp.float32)
    others = squares_refs[0][line : line + 1, :]
    for ref in squares_refs[1:]:
        others = others + ref[line : line + 1, :]
    squares = jnp.broadcast_to(others, (seq, seq)).T + jnp.sum(
        values * values, axis=-1, keepdims=True
    )
    scale = lax.rsqrt(squares / WIDTH + EPSILON)
    lane_group = lax.broadcasted_iota(jnp.int32, (seq, LANES), 1) // GROUP_SIZE
    for block in range(channels // LANES):
        lanes = slice(block * LANES, (block + 1) * LANES)
        normed = values[:, lanes] * scale * gains_ref[:, lanes]
        narrow = normed.astype(jnp.bfloat16)
        spread = jnp.concatenate(
            [
                jnp.where(lane_group == part, narrow, jnp.zeros_like(narrow))
                for part in range(PER_BLOCK)
            ],
            axis=0,
        )
        mixed = jnp.dot(blocks_ref[block], spread, preferred_element_type=jnp.float32)
        gated_buf[:, lanes] = (normed * mixed).astype(jnp.bfloat16)
    for apart in reversed(range(count)):
        start = pl.multiple_of((place ^ apart) * channels, channels)
        out_refs[apart][...] = jnp.dot(
            gated_buf[...],
            weight_ref[:, pl.ds(start, channels)],
            preferred_element_type=jnp.float32,
        ).astype(out_refs[apart].dtype)


def layer_partials(x, squares, line, gains, blocks, weight, count, after):
    seq, channels = x.shape
    kinds = [jnp.bfloat16 if apart % 2 else jnp.float32 for apart in range(count)]
    return pl.pallas_call(
        functools.partial(layer_kernel, count, line),
        out_shape=[jax.ShapeDtypeStruct((seq, channels), kind) for kind in kinds],
        in_specs=[IN_VMEM] * (3 + count) + [IN_PLACE] * len(after),
        out_specs=[IN_VMEM] * count,
        scratch_shapes=[pltpu.VMEM((seq, channels), jnp.bfloat16)],
        compiler_params=pltpu.CompilerParams(vmem_limit_bytes=12 * 2**20),
        cost_estimate=pl.CostEstimate(
            flops=1 * 2 * seq * channels * channels * count,
            transcendentals=0,
            bytes_accessed=1 * 2 * channels * channels * count,
        ),
        name="layer",
    )(x, gains, blocks, weight, *squares, *after)


def section_output(x_ref, own_ref, arrived):
    total = own_ref[...]
    for ref in arrived:
        total = total + ref[...].astype(jnp.float32)
    return (x_ref[...].astype(jnp.float32) + total).astype(jnp.bfloat16)


def merge_kernel(count, x_ref, fresh_ref, own_ref, *refs):
    arrived, (y_ref, sent_ref, squares_ref) = refs[:count], refs[-3:]
    y = section_output(x_ref, own_ref, arrived)
    y_ref[...] = y
    last = lax.axis_index("pipe") == lax.axis_size("pipe") - 1
    sent = jnp.where(last, fresh_ref[...].astype(jnp.float32), y.astype(jnp.float32))
    sent_ref[...] = sent.astype(jnp.bfloat16)
    squares_ref[...] = row_squares(sent)


def merge(x, fresh, own, arrived, after):
    seq, channels = x.shape
    return pl.pallas_call(
        functools.partial(merge_kernel, len(arrived)),
        out_shape=[
            jax.ShapeDtypeStruct((seq, channels), jnp.bfloat16),
            jax.ShapeDtypeStruct((seq, channels), jnp.bfloat16),
            jax.ShapeDtypeStruct((1, seq), jnp.float32),
        ],
        in_specs=[IN_VMEM] * (3 + len(arrived)) + [IN_PLACE] * len(after),
        out_specs=[IN_VMEM] * 3,
        compiler_params=pltpu.CompilerParams(vmem_limit_bytes=6 * 2**20),
        name="merge",
    )(x, fresh, own, *arrived, *after)


def end_kernel(count, x_ref, own_ref, *refs):
    refs[-1][...] = section_output(x_ref, own_ref, refs[:count])


def end(x, own, arrived, after):
    return pl.pallas_call(
        functools.partial(end_kernel, len(arrived)),
        out_shape=jax.ShapeDtypeStruct(x.shape, jnp.bfloat16),
        in_specs=[IN_VMEM] * (2 + len(arrived)) + [IN_PLACE] * len(after),
        out_specs=IN_VMEM,
        compiler_params=pltpu.CompilerParams(vmem_limit_bytes=6 * 2**20),
        name="end",
    )(x, own, *arrived, *after)


def collect_kernel(count, spots, x_ref, own_ref, *refs):
    arrived, earlier, (all_ref, y_ref, sems) = refs[:count], refs[count:-3], refs[-3:]
    targets = [all_ref.at[tick, way, 0] for tick, way in spots]
    copies = [
        pltpu.make_async_copy(source, target, sems.at[spot])
        for spot, (source, target) in enumerate(zip([*earlier, y_ref], targets))
    ]
    for copy in copies[:-1]:
        copy.start()
    y_ref[...] = section_output(x_ref, own_ref, arrived)
    copies[-1].start()
    for copy in copies:
        copy.wait()


def collect(x, own, arrived, earlier, spots):
    return pl.pallas_call(
        functools.partial(collect_kernel, len(arrived), spots),
        out_shape=jax.ShapeDtypeStruct((TICK_COUNT, 2, 1, *x.shape), jnp.bfloat16),
        in_specs=[IN_VMEM] * (2 + len(arrived)) + [IN_PLACE] * len(earlier),
        out_specs=IN_PLACE,
        scratch_shapes=[
            pltpu.VMEM(x.shape, jnp.bfloat16),
            pltpu.SemaphoreType.DMA((len(spots),)),
        ],
        compiler_params=pltpu.CompilerParams(vmem_limit_bytes=6 * 2**20),
        name="collect",
    )(x, own, *arrived, *earlier)


def send(values, target):
    pipe, tensor = lax.axis_size("pipe"), lax.axis_size("tensor")
    pairs = []
    for k in range(pipe):
        for z in range(tensor):
            to_k, to_z = target(k, z)
            pairs.append((k * tensor + z, to_k * tensor + to_z))
    return lax.ppermute(values, ("pipe", "tensor"), pairs)


def first_halving(partials, after):
    partials = list(partials)
    for apart in reversed(range(3, len(partials), 2)):
        incoming = send(partials[apart], lambda k, z: (k, z ^ 1))
        incoming, after = lax.optimization_barrier((incoming, after))
        partials[apart ^ 1] = partials[apart ^ 1] + incoming.astype(jnp.float32)
    kept = partials[:2] + [
        partial.astype(jnp.bfloat16) if apart == 2 else partial
        for apart, partial in enumerate(partials)
        if apart >= 2 and apart % 2 == 0
    ]
    return kept, after


def other_halvings(partials):
    pair, rest = partials[:2], partials[2:]
    arrived = []
    left = {2 * (spot + 1): partial for spot, partial in enumerate(rest)}
    bit = 2
    while left:
        for apart in sorted(left, reverse=True):
            if apart & bit:
                incoming = send(
                    left.pop(apart).astype(jnp.bfloat16), lambda k, z: (k, z ^ bit)
                )
                if apart == bit:
                    arrived.append(incoming)
                else:
                    left[apart ^ bit] = left[apart ^ bit].astype(jnp.float32) + incoming.astype(
                        jnp.float32
                    )
        bit *= 2
    return arrived + [send(pair[1], lambda k, z: (k, z ^ 1))]


def local(
    down_state, up_state, layer_proj, conv_filters, norm_gains, embedding, dna_tokens, entry_order
):
    pipe, tensor = lax.axis_size("pipe"), lax.axis_size("tensor")
    gains = norm_gains

    def mirrored(k):
        return pipe - 1 - k

    def following(k):
        return (k + 1) % pipe

    def spread(sums, target):
        return [
            send(sums, lambda k, z, apart=apart: (target(k), z ^ apart))
            for apart in range(1, tensor)
        ]

    down, up = 0, 1
    entering = [down_state[0], up_state[0]]
    sums = squares_of(*entering)
    squares = [spread(sums, lambda k: k), spread(sums, mirrored)]
    entering[up] = send(entering[up], lambda k, z: (mirrored(k), z))
    blocks, weight, fresh = prepare(
        conv_filters[0], layer_proj[0], dna_tokens, entry_order, embedding
    )

    def go_on(partials):
        own, *rest = partials
        rest = lax.optimization_barrier(rest)
        return own, other_halvings([own, *rest]), rest[1:2]

    def run_layer(way, tick, after):
        *partials, neighbour = layer_partials(
            entering[way],
            squares[way],
            way if tick == 0 else 0,
            gains,
            blocks,
            weight,
            tensor,
            after,
        )
        if (way, tick) in ((up, 1), (down, 2)):
            neighbour, y = lax.optimization_barrier((neighbour, leaving[up].pop()))
            leaving[up].append(send(y, lambda k, z: (mirrored(k), z)))
        return [*partials, neighbour]

    def finish(way, tick, own, arrived):
        after = leaving[up][-1:] if (way, tick) in ((down, 0), (up, 2)) else []
        if tick == TICK_COUNT - 1:
            leaving[way].append(end(entering[way], own, arrived, after))
            return
        y, sent, sums = merge(entering[way], fresh[way][tick], own, arrived, after)
        leaving[way].append(y)
        entering[way] = send(sent, lambda k, z: (following(k), z))
        squares[way] = spread(sums, following)

    leaving = [[], []]
    partials, _ = first_halving(run_layer(up, 0, []), [])
    own, arrived, early = go_on(partials)
    for turn in range(1, 2 * TICK_COUNT):
        way, tick = (up, down)[turn % 2], turn // 2
        partials = run_layer(way, tick, early)
        finish(1 - way, (turn - 1) // 2, own, arrived)
        ending = turn == 2 * TICK_COUNT - 1
        held = [leaving[up].pop()] if ending else []
        partials, held = first_halving(partials, held)
        leaving[up].extend(held)
        own, arrived, early = go_on(partials)
    leaving[up].append(send(leaving[up].pop(), lambda k, z: (mirrored(k), z)))
    earlier = [*leaving[down], *leaving[up]]
    spots = [(tick, down) for tick in range(TICK_COUNT - 1)]
    spots += [(tick, up) for tick in range(TICK_COUNT)] + [(TICK_COUNT - 1, down)]
    return collect(entering[down], own, arrived, earlier, spots)


def solution(mesh):
    placed = (
        P("pipe", None, "tensor"),
        P("pipe", None, "tensor"),
        P("pipe", "tensor", None),
        P("pipe", "tensor", None),
        P("pipe", "tensor"),
        P(None, "tensor"),
        P(),
        P(),
    )
    return jax.shard_map(
        local,
        mesh=mesh,
        in_specs=placed,
        out_specs=P(None, None, "pipe", None, "tensor"),
        check_vma=False,
    )
```

```python
import functools

import jax
import jax.numpy as jnp
from jax import lax
from jax.experimental import pallas as pl
from jax.experimental.pallas import tpu as pltpu
from jax.sharding import PartitionSpec as P

WIDTH = 4096
SHORT_TAPS = 7
LONG_TAPS = 128
GROUP_SIZE = 16
TICK_COUNT = 3
EPSILON = 1e-06

LANES = 128
PER_BLOCK = LANES // GROUP_SIZE
IN_VMEM = pl.BlockSpec(memory_space=pltpu.VMEM)
IN_PLACE = pl.BlockSpec(memory_space=pl.ANY)


def halves(values):
    high = values.astype(jnp.bfloat16)
    return high, (values - high.astype(jnp.float32)).astype(jnp.bfloat16)


def prepare_kernel(
    ticks, order_hbm, filters_hbm, tokens_hbm, table_hbm, weight_hbm, *refs
):
    blocks_ref, weight_ref, refs = refs[0], refs[1], refs[2:]
    fresh_refs, refs = refs[: 2 * ticks], refs[2 * ticks :]
    order_ref, filters_ref, tokens_ref, table_ref, sems = refs
    copies = [
        pltpu.make_async_copy(source, target, sems.at[spot])
        for spot, (source, target) in enumerate(
            [
                (filters_hbm, filters_ref),
                (order_hbm, order_ref),
                (tokens_hbm, tokens_ref),
                (table_hbm, table_ref),
                (weight_hbm, weight_ref),
            ]
        )
    ]
    for copy in copies:
        copy.start()
    copies[0].wait()
    groups, seq = filters_ref.shape
    taps = jnp.where(lax.axis_index("pipe") % 2 == 0, SHORT_TAPS, LONG_TAPS)
    lane = lax.broadcasted_iota(jnp.int32, (groups, seq), 1)
    kept = jnp.where(lane < taps, filters_ref[...], 0.0)
    row = lax.broadcasted_iota(jnp.int32, (seq, seq), 0)
    col = lax.broadcasted_iota(jnp.int32, (seq, seq), 1)
    flip = ((row + col) % seq == 0).astype(jnp.bfloat16)
    backward = sum(
        jnp.dot(part, flip, preferred_element_type=jnp.float32) for part in halves(kept)
    )
    for group in range(groups):
        wide = jnp.broadcast_to(backward[group : group + 1, :], (seq, seq))
        turned = pltpu.roll(wide, 0, 1, stride=1, stride_axis=0)
        start = group % PER_BLOCK * seq
        for half, part in enumerate(halves(jnp.where(row >= col, turned, 0.0))):
            blocks_ref[group // PER_BLOCK, half, :, start : start + seq] = part
    for copy in copies[1:4]:
        copy.wait()
    word = lax.broadcasted_iota(jnp.int32, (table_ref.shape[0], seq), 0)
    for entry, fresh_ref in enumerate(fresh_refs):
        way, tick = entry // ticks, entry % ticks
        chosen = tokens_ref[way, pl.ds(order_ref[way, tick], 1), :]
        onehot = (word == chosen).astype(jnp.bfloat16)
        fresh_ref[...] = lax.dot_general(
            onehot, table_ref[...], (((0,), (0,)), ((), ())), preferred_element_type=jnp.float32
        ).astype(fresh_ref.dtype)
    copies[4].wait()


def in_hbm(array):
    return pltpu.with_memory_space_constraint(array, pltpu.HBM)


def prepare(filters, weight, tokens, order, table):
    groups, seq = filters.shape
    ticks = TICK_COUNT - 1
    blocks, held, *fresh = pl.pallas_call(
        functools.partial(prepare_kernel, ticks),
        out_shape=[
            jax.ShapeDtypeStruct((groups // PER_BLOCK, 2, seq, PER_BLOCK * seq), jnp.bfloat16),
            jax.ShapeDtypeStruct(weight.shape, weight.dtype),
        ]
        + [jax.ShapeDtypeStruct((seq, table.shape[1]), table.dtype)] * (2 * ticks),
        in_specs=[IN_PLACE] * 5,
        out_specs=[IN_VMEM] * (2 + 2 * ticks),
        scratch_shapes=[
            pltpu.SMEM(order.shape, order.dtype),
            pltpu.VMEM(filters.shape, filters.dtype),
            pltpu.VMEM(tokens.shape, tokens.dtype),
            pltpu.VMEM(table.shape, table.dtype),
            pltpu.SemaphoreType.DMA((5,)),
        ],
        compiler_params=pltpu.CompilerParams(vmem_limit_bytes=20 * 2**20),
        name="prepare",
    )(in_hbm(order), in_hbm(filters), in_hbm(tokens), in_hbm(table), in_hbm(weight))
    return blocks, held, [fresh[:ticks], fresh[ticks:]]


def row_squares(values):
    seq, channels = values.shape
    squares = values * values
    total = squares[:, :LANES]
    for start in range(LANES, channels, LANES):
        total = total + squares[:, start : start + LANES]
    return jnp.sum(total.T, axis=0, keepdims=True)


def squares_kernel(count, *refs):
    sources, squares_ref, held_ref, sems = refs[:count], refs[-3], refs[-2], refs[-1]
    copies = [
        pltpu.make_async_copy(source, held_ref.at[spot], sems.at[spot])
        for spot, source in enumerate(sources)
    ]
    for copy in copies:
        copy.start()
    for spot, copy in enumerate(copies):
        copy.wait()
        squares_ref[spot : spot + 1, :] = row_squares(held_ref[spot].astype(jnp.float32))


def squares_of(*arrays):
    count = len(arrays)
    return pl.pallas_call(
        functools.partial(squares_kernel, count),
        out_shape=jax.ShapeDtypeStruct((count, arrays[0].shape[0]), jnp.float32),
        in_specs=[IN_PLACE] * count,
        out_specs=IN_VMEM,
        scratch_shapes=[
            pltpu.VMEM((count, *arrays[0].shape), arrays[0].dtype),
            pltpu.SemaphoreType.DMA((count,)),
        ],
        compiler_params=pltpu.CompilerParams(vmem_limit_bytes=6 * 2**20),
        name="squares",
    )(*[in_hbm(array) for array in arrays])


def layer_kernel(count, line, x_ref, gains_ref, blocks_ref, weight_ref, *refs):
    squares_refs, out_refs, gated_buf = refs[: count - 1], refs[-count - 1 : -1], refs[-1]
    place = lax.axis_index("tensor")
    seq, channels = x_ref.shape
    values = x_ref[...].astype(jnp.float32)
    others = squares_refs[0][line : line + 1, :]
    for ref in squares_refs[1:]:
        others = others + ref[line : line + 1, :]
    squares = jnp.broadcast_to(others, (seq, seq)).T + jnp.sum(
        values * values, axis=-1, keepdims=True
    )
    scale = lax.rsqrt(squares / WIDTH + EPSILON)
    lane_group = lax.broadcasted_iota(jnp.int32, (seq, LANES), 1) // GROUP_SIZE
    for block in range(channels // LANES):
        lanes = slice(block * LANES, (block + 1) * LANES)
        normed = values[:, lanes] * scale * gains_ref[:, lanes]
        high, low = [
            jnp.concatenate(
                [
                    jnp.where(lane_group == part, half, jnp.zeros_like(half))
                    for part in range(PER_BLOCK)
                ],
                axis=0,
            )
            for half in halves(normed)
        ]
        mixed = (
            jnp.dot(blocks_ref[block, 0], high, preferred_element_type=jnp.float32)
            + jnp.dot(blocks_ref[block, 1], high, preferred_element_type=jnp.float32)
            + jnp.dot(blocks_ref[block, 0], low, preferred_element_type=jnp.float32)
        )
        gated_buf[:, lanes] = (normed * mixed).astype(jnp.bfloat16)
    for apart in reversed(range(count)):
        start = pl.multiple_of((place ^ apart) * channels, channels)
        out_refs[apart][...] = jnp.dot(
            gated_buf[...],
            weight_ref[:, pl.ds(start, channels)],
            preferred_element_type=jnp.float32,
        ).astype(out_refs[apart].dtype)


def layer_partials(x, squares, line, gains, blocks, weight, count, after):
    seq, channels = x.shape
    kinds = [jnp.bfloat16 if apart % 2 else jnp.float32 for apart in range(count)]
    return pl.pallas_call(
        functools.partial(layer_kernel, count, line),
        out_shape=[jax.ShapeDtypeStruct((seq, channels), kind) for kind in kinds],
        in_specs=[IN_VMEM] * (3 + count) + [IN_PLACE] * len(after),
        out_specs=[IN_VMEM] * count,
        scratch_shapes=[pltpu.VMEM((seq, channels), jnp.bfloat16)],
        compiler_params=pltpu.CompilerParams(vmem_limit_bytes=16 * 2**20),
        cost_estimate=pl.CostEstimate(
            flops=1 * 2 * seq * channels * channels * count,
            transcendentals=0,
            bytes_accessed=1 * 2 * channels * channels * count,
        ),
        name="layer",
    )(x, gains, blocks, weight, *squares, *after)


def section_output(x_ref, own_ref, arrived):
    total = own_ref[...]
    for ref in arrived:
        total = total + ref[...].astype(jnp.float32)
    return (x_ref[...].astype(jnp.float32) + total).astype(jnp.bfloat16)


def merge_kernel(count, x_ref, fresh_ref, own_ref, *refs):
    arrived, (y_ref, sent_ref, squares_ref) = refs[:count], refs[-3:]
    y = section_output(x_ref, own_ref, arrived)
    y_ref[...] = y
    last = lax.axis_index("pipe") == lax.axis_size("pipe") - 1
    sent = jnp.where(last, fresh_ref[...].astype(jnp.float32), y.astype(jnp.float32))
    sent_ref[...] = sent.astype(jnp.bfloat16)
    squares_ref[...] = row_squares(sent)


def merge(x, fresh, own, arrived, after):
    seq, channels = x.shape
    return pl.pallas_call(
        functools.partial(merge_kernel, len(arrived)),
        out_shape=[
            jax.ShapeDtypeStruct((seq, channels), jnp.bfloat16),
            jax.ShapeDtypeStruct((seq, channels), jnp.bfloat16),
            jax.ShapeDtypeStruct((1, seq), jnp.float32),
        ],
        in_specs=[IN_VMEM] * (3 + len(arrived)) + [IN_PLACE] * len(after),
        out_specs=[IN_VMEM] * 3,
        compiler_params=pltpu.CompilerParams(vmem_limit_bytes=6 * 2**20),
        name="merge",
    )(x, fresh, own, *arrived, *after)


def end_kernel(count, x_ref, own_ref, *refs):
    refs[-1][...] = section_output(x_ref, own_ref, refs[:count])


def end(x, own, arrived, after):
    return pl.pallas_call(
        functools.partial(end_kernel, len(arrived)),
        out_shape=jax.ShapeDtypeStruct(x.shape, jnp.bfloat16),
        in_specs=[IN_VMEM] * (2 + len(arrived)) + [IN_PLACE] * len(after),
        out_specs=IN_VMEM,
        compiler_params=pltpu.CompilerParams(vmem_limit_bytes=6 * 2**20),
        name="end",
    )(x, own, *arrived, *after)


def collect_kernel(count, spots, x_ref, own_ref, *refs):
    arrived, earlier, (all_ref, y_ref, sems) = refs[:count], refs[count:-3], refs[-3:]
    targets = [all_ref.at[tick, way, 0] for tick, way in spots]
    copies = [
        pltpu.make_async_copy(source, target, sems.at[spot])
        for spot, (source, target) in enumerate(zip([*earlier, y_ref], targets))
    ]
    for copy in copies[:-1]:
        copy.start()
    y_ref[...] = section_output(x_ref, own_ref, arrived)
    copies[-1].start()
    for copy in copies:
        copy.wait()


def collect(x, own, arrived, earlier, spots):
    return pl.pallas_call(
        functools.partial(collect_kernel, len(arrived), spots),
        out_shape=jax.ShapeDtypeStruct((TICK_COUNT, 2, 1, *x.shape), jnp.bfloat16),
        in_specs=[IN_VMEM] * (2 + len(arrived)) + [IN_PLACE] * len(earlier),
        out_specs=IN_PLACE,
        scratch_shapes=[
            pltpu.VMEM(x.shape, jnp.bfloat16),
            pltpu.SemaphoreType.DMA((len(spots),)),
        ],
        compiler_params=pltpu.CompilerParams(vmem_limit_bytes=6 * 2**20),
        name="collect",
    )(x, own, *arrived, *earlier)


def send(values, target):
    pipe, tensor = lax.axis_size("pipe"), lax.axis_size("tensor")
    pairs = []
    for k in range(pipe):
        for z in range(tensor):
            to_k, to_z = target(k, z)
            pairs.append((k * tensor + z, to_k * tensor + to_z))
    return lax.ppermute(values, ("pipe", "tensor"), pairs)


def first_halving(partials, after):
    partials = list(partials)
    for apart in reversed(range(3, len(partials), 2)):
        incoming = send(partials[apart], lambda k, z: (k, z ^ 1))
        incoming, after = lax.optimization_barrier((incoming, after))
        partials[apart ^ 1] = partials[apart ^ 1] + incoming.astype(jnp.float32)
    kept = partials[:2] + [
        partial.astype(jnp.bfloat16) if apart == 2 else partial
        for apart, partial in enumerate(partials)
        if apart >= 2 and apart % 2 == 0
    ]
    return kept, after


def other_halvings(partials):
    pair, rest = partials[:2], partials[2:]
    arrived = []
    left = {2 * (spot + 1): partial for spot, partial in enumerate(rest)}
    bit = 2
    while left:
        for apart in sorted(left, reverse=True):
            if apart & bit:
                incoming = send(
                    left.pop(apart).astype(jnp.bfloat16), lambda k, z: (k, z ^ bit)
                )
                if apart == bit:
                    arrived.append(incoming)
                else:
                    left[apart ^ bit] = left[apart ^ bit].astype(jnp.float32) + incoming.astype(
                        jnp.float32
                    )
        bit *= 2
    return arrived + [send(pair[1], lambda k, z: (k, z ^ 1))]


def local(
    down_state, up_state, layer_proj, conv_filters, norm_gains, embedding, dna_tokens, entry_order
):
    pipe, tensor = lax.axis_size("pipe"), lax.axis_size("tensor")
    gains = norm_gains

    def mirrored(k):
        return pipe - 1 - k

    def following(k):
        return (k + 1) % pipe

    def spread(sums, target):
        return [
            send(sums, lambda k, z, apart=apart: (target(k), z ^ apart))
            for apart in range(1, tensor)
        ]

    down, up = 0, 1
    entering = [down_state[0], up_state[0]]
    sums = squares_of(*entering)
    entering[up], sums = lax.optimization_barrier((entering[up], sums))
    entering[up] = send(entering[up], lambda k, z: (mirrored(k), z))
    squares = [spread(sums, lambda k: k), spread(sums, mirrored)]
    blocks, weight, fresh = prepare(
        conv_filters[0], layer_proj[0], dna_tokens, entry_order, embedding
    )

    def go_on(partials):
        own, *rest = partials
        rest = lax.optimization_barrier(rest)
        return own, other_halvings([own, *rest]), rest[1:2]

    def run_layer(way, tick, after):
        *partials, neighbour = layer_partials(
            entering[way],
            squares[way],
            way if tick == 0 else 0,
            gains,
            blocks,
            weight,
            tensor,
            after,
        )
        if (way, tick) in ((up, 1), (down, 2)):
            neighbour, y = lax.optimization_barrier((neighbour, leaving[up].pop()))
            leaving[up].append(send(y, lambda k, z: (mirrored(k), z)))
        return [*partials, neighbour]

    def finish(way, tick, own, arrived):
        after = leaving[up][-1:] if (way, tick) in ((down, 0), (up, 2)) else []
        if tick == TICK_COUNT - 1:
            leaving[way].append(end(entering[way], own, arrived, after))
            return
        y, sent, sums = merge(entering[way], fresh[way][tick], own, arrived, after)
        leaving[way].append(y)
        entering[way] = send(sent, lambda k, z: (following(k), z))
        squares[way] = spread(sums, following)

    leaving = [[], []]
    partials, _ = first_halving(run_layer(up, 0, []), [])
    own, arrived, early = go_on(partials)
    for turn in range(1, 2 * TICK_COUNT):
        way, tick = (up, down)[turn % 2], turn // 2
        partials = run_layer(way, tick, early)
        finish(1 - way, (turn - 1) // 2, own, arrived)
        ending = turn == 2 * TICK_COUNT - 1
        held = [leaving[up].pop()] if ending else []
        partials, held = first_halving(partials, held)
        leaving[up].extend(held)
        own, arrived, early = go_on(partials)
    leaving[up].append(send(leaving[up].pop(), lambda k, z: (mirrored(k), z)))
    earlier = [*leaving[down], *leaving[up]]
    spots = [(tick, down) for tick in range(TICK_COUNT - 1)]
    spots += [(tick, up) for tick in range(TICK_COUNT)] + [(TICK_COUNT - 1, down)]
    return collect(entering[down], own, arrived, earlier, spots)


def solution(mesh):
    placed = (
        P("pipe", None, "tensor"),
        P("pipe", None, "tensor"),
        P("pipe", "tensor", None),
        P("pipe", "tensor", None),
        P("pipe", "tensor"),
        P(None, "tensor"),
        P(),
        P(),
    )
    return jax.shard_map(
        local,
        mesh=mesh,
        in_specs=placed,
        out_specs=P(None, None, "pipe", None, "tensor"),
        check_vma=False,
    )
```

```python
import functools

import jax
import jax.numpy as jnp
from jax import lax
from jax.experimental import pallas as pl
from jax.experimental.pallas import tpu as pltpu
from jax.sharding import PartitionSpec as P

WIDTH = 4096
SHORT_TAPS = 7
LONG_TAPS = 128
GROUP_SIZE = 16
TICK_COUNT = 3
EPSILON = 1e-06

LANES = 128
PER_BLOCK = LANES // GROUP_SIZE
IN_VMEM = pl.BlockSpec(memory_space=pltpu.VMEM)
IN_PLACE = pl.BlockSpec(memory_space=pl.ANY)


def halves(values):
    high = values.astype(jnp.bfloat16)
    return high, (values - high.astype(jnp.float32)).astype(jnp.bfloat16)


def prepare_kernel(
    ticks, order_hbm, filters_hbm, tokens_hbm, table_hbm, weight_hbm, *refs
):
    blocks_ref, weight_ref, refs = refs[0], refs[1], refs[2:]
    fresh_refs, refs = refs[: 2 * ticks], refs[2 * ticks :]
    order_ref, filters_ref, tokens_ref, table_ref, sems = refs
    copies = [
        pltpu.make_async_copy(source, target, sems.at[spot])
        for spot, (source, target) in enumerate(
            [
                (filters_hbm, filters_ref),
                (order_hbm, order_ref),
                (tokens_hbm, tokens_ref),
                (table_hbm, table_ref),
                (weight_hbm, weight_ref),
            ]
        )
    ]
    for copy in copies:
        copy.start()
    copies[0].wait()
    groups, seq = filters_ref.shape
    taps = jnp.where(lax.axis_index("pipe") % 2 == 0, SHORT_TAPS, LONG_TAPS)
    lane = lax.broadcasted_iota(jnp.int32, (groups, seq), 1)
    kept = jnp.where(lane < taps, filters_ref[...], 0.0)
    row = lax.broadcasted_iota(jnp.int32, (seq, seq), 0)
    col = lax.broadcasted_iota(jnp.int32, (seq, seq), 1)
    flip = ((row + col) % seq == 0).astype(jnp.bfloat16)
    backward = sum(
        jnp.dot(part, flip, preferred_element_type=jnp.float32) for part in halves(kept)
    )
    for group in range(groups):
        wide = jnp.broadcast_to(backward[group : group + 1, :], (seq, seq))
        turned = pltpu.roll(wide, 0, 1, stride=1, stride_axis=0)
        start = group % PER_BLOCK * seq
        for half, part in enumerate(halves(jnp.where(row >= col, turned, 0.0))):
            blocks_ref[group // PER_BLOCK, half, :, start : start + seq] = part
    for copy in copies[1:4]:
        copy.wait()
    word = lax.broadcasted_iota(jnp.int32, (table_ref.shape[0], seq), 0)
    for entry, fresh_ref in enumerate(fresh_refs):
        way, tick = entry // ticks, entry % ticks
        chosen = tokens_ref[way, pl.ds(order_ref[way, tick], 1), :]
        onehot = (word == chosen).astype(jnp.bfloat16)
        fresh_ref[...] = lax.dot_general(
            onehot, table_ref[...], (((0,), (0,)), ((), ())), preferred_element_type=jnp.float32
        ).astype(fresh_ref.dtype)
    copies[4].wait()


def in_hbm(array):
    return pltpu.with_memory_space_constraint(array, pltpu.HBM)


def prepare(filters, weight, tokens, order, table):
    groups, seq = filters.shape
    ticks = TICK_COUNT - 1
    blocks, held, *fresh = pl.pallas_call(
        functools.partial(prepare_kernel, ticks),
        out_shape=[
            jax.ShapeDtypeStruct((groups // PER_BLOCK, 2, seq, PER_BLOCK * seq), jnp.bfloat16),
            jax.ShapeDtypeStruct(weight.shape, weight.dtype),
        ]
        + [jax.ShapeDtypeStruct((seq, table.shape[1]), table.dtype)] * (2 * ticks),
        in_specs=[IN_PLACE] * 5,
        out_specs=[IN_VMEM] * (2 + 2 * ticks),
        scratch_shapes=[
            pltpu.SMEM(order.shape, order.dtype),
            pltpu.VMEM(filters.shape, filters.dtype),
            pltpu.VMEM(tokens.shape, tokens.dtype),
            pltpu.VMEM(table.shape, table.dtype),
            pltpu.SemaphoreType.DMA((5,)),
        ],
        compiler_params=pltpu.CompilerParams(vmem_limit_bytes=20 * 2**20),
        name="prepare",
    )(in_hbm(order), in_hbm(filters), in_hbm(tokens), in_hbm(table), in_hbm(weight))
    return blocks, held, [fresh[:ticks], fresh[ticks:]]


def row_squares(values):
    seq, channels = values.shape
    squares = values * values
    total = squares[:, :LANES]
    for start in range(LANES, channels, LANES):
        total = total + squares[:, start : start + LANES]
    return jnp.sum(total.T, axis=0, keepdims=True)


def squares_kernel(count, *refs):
    sources, squares_ref, held_ref, sems = refs[:count], refs[-3], refs[-2], refs[-1]
    copies = [
        pltpu.make_async_copy(source, held_ref.at[spot], sems.at[spot])
        for spot, source in enumerate(sources)
    ]
    for copy in copies:
        copy.start()
    for spot, copy in enumerate(copies):
        copy.wait()
        squares_ref[spot : spot + 1, :] = row_squares(held_ref[spot].astype(jnp.float32))


def squares_of(*arrays):
    count = len(arrays)
    return pl.pallas_call(
        functools.partial(squares_kernel, count),
        out_shape=jax.ShapeDtypeStruct((count, arrays[0].shape[0]), jnp.float32),
        in_specs=[IN_PLACE] * count,
        out_specs=IN_VMEM,
        scratch_shapes=[
            pltpu.VMEM((count, *arrays[0].shape), arrays[0].dtype),
            pltpu.SemaphoreType.DMA((count,)),
        ],
        compiler_params=pltpu.CompilerParams(vmem_limit_bytes=6 * 2**20),
        name="squares",
    )(*[in_hbm(array) for array in arrays])


def layer_kernel(count, line, x_ref, gains_ref, blocks_ref, weight_ref, *refs):
    squares_refs, out_refs, gated_buf = refs[: count - 1], refs[-count - 1 : -1], refs[-1]
    place = lax.axis_index("tensor")
    seq, channels = x_ref.shape
    values = x_ref[...].astype(jnp.float32)
    others = squares_refs[0][line : line + 1, :]
    for ref in squares_refs[1:]:
        others = others + ref[line : line + 1, :]
    squares = jnp.broadcast_to(others, (seq, seq)).T + jnp.sum(
        values * values, axis=-1, keepdims=True
    )
    scale = lax.rsqrt(squares / WIDTH + EPSILON)
    lane_group = lax.broadcasted_iota(jnp.int32, (seq, LANES), 1) // GROUP_SIZE
    for block in range(channels // LANES):
        lanes = slice(block * LANES, (block + 1) * LANES)
        normed = values[:, lanes] * scale * gains_ref[:, lanes]
        high, low = [
            jnp.concatenate(
                [
                    jnp.where(lane_group == part, half, jnp.zeros_like(half))
                    for part in range(PER_BLOCK)
                ],
                axis=0,
            )
            for half in halves(normed)
        ]
        filters = blocks_ref[block].reshape(2 * seq, PER_BLOCK * seq)
        parts = jnp.dot(
            filters, jnp.concatenate([high, low], axis=1), preferred_element_type=jnp.float32
        )
        mixed = parts[:seq, :LANES] + (parts[seq:, :LANES] + parts[:seq, LANES:])
        gated_buf[:, lanes] = (normed * mixed).astype(jnp.bfloat16)
    for apart in reversed(range(count)):
        start = pl.multiple_of((place ^ apart) * channels, channels)
        out_refs[apart][...] = jnp.dot(
            gated_buf[...],
            weight_ref[:, pl.ds(start, channels)],
            preferred_element_type=jnp.float32,
        ).astype(out_refs[apart].dtype)


def layer_partials(x, squares, line, gains, blocks, weight, count, after):
    seq, channels = x.shape
    kinds = [jnp.bfloat16 if apart % 2 else jnp.float32 for apart in range(count)]
    return pl.pallas_call(
        functools.partial(layer_kernel, count, line),
        out_shape=[jax.ShapeDtypeStruct((seq, channels), kind) for kind in kinds],
        in_specs=[IN_VMEM] * (3 + count) + [IN_PLACE] * len(after),
        out_specs=[IN_VMEM] * count,
        scratch_shapes=[pltpu.VMEM((seq, channels), jnp.bfloat16)],
        compiler_params=pltpu.CompilerParams(vmem_limit_bytes=16 * 2**20),
        cost_estimate=pl.CostEstimate(
            flops=1 * 2 * seq * channels * channels * count,
            transcendentals=0,
            bytes_accessed=1 * 2 * channels * channels * count,
        ),
        name="layer",
    )(x, gains, blocks, weight, *squares, *after)


def section_output(x_ref, own_ref, arrived):
    total = own_ref[...]
    for ref in arrived:
        total = total + ref[...].astype(jnp.float32)
    return (x_ref[...].astype(jnp.float32) + total).astype(jnp.bfloat16)


def merge_kernel(count, x_ref, fresh_ref, own_ref, *refs):
    arrived, (y_ref, sent_ref, squares_ref) = refs[:count], refs[-3:]
    y = section_output(x_ref, own_ref, arrived)
    y_ref[...] = y
    last = lax.axis_index("pipe") == lax.axis_size("pipe") - 1
    sent = jnp.where(last, fresh_ref[...].astype(jnp.float32), y.astype(jnp.float32))
    sent_ref[...] = sent.astype(jnp.bfloat16)
    squares_ref[...] = row_squares(sent)


def merge(x, fresh, own, arrived, after):
    seq, channels = x.shape
    return pl.pallas_call(
        functools.partial(merge_kernel, len(arrived)),
        out_shape=[
            jax.ShapeDtypeStruct((seq, channels), jnp.bfloat16),
            jax.ShapeDtypeStruct((seq, channels), jnp.bfloat16),
            jax.ShapeDtypeStruct((1, seq), jnp.float32),
        ],
        in_specs=[IN_VMEM] * (3 + len(arrived)) + [IN_PLACE] * len(after),
        out_specs=[IN_VMEM] * 3,
        compiler_params=pltpu.CompilerParams(vmem_limit_bytes=6 * 2**20),
        name="merge",
    )(x, fresh, own, *arrived, *after)


def end_kernel(count, x_ref, own_ref, *refs):
    refs[-1][...] = section_output(x_ref, own_ref, refs[:count])


def end(x, own, arrived, after):
    return pl.pallas_call(
        functools.partial(end_kernel, len(arrived)),
        out_shape=jax.ShapeDtypeStruct(x.shape, jnp.bfloat16),
        in_specs=[IN_VMEM] * (2 + len(arrived)) + [IN_PLACE] * len(after),
        out_specs=IN_VMEM,
        compiler_params=pltpu.CompilerParams(vmem_limit_bytes=6 * 2**20),
        name="end",
    )(x, own, *arrived, *after)


def collect_kernel(count, spots, x_ref, own_ref, *refs):
    arrived, earlier, (all_ref, y_ref, sems) = refs[:count], refs[count:-3], refs[-3:]
    targets = [all_ref.at[tick, way, 0] for tick, way in spots]
    copies = [
        pltpu.make_async_copy(source, target, sems.at[spot])
        for spot, (source, target) in enumerate(zip([*earlier, y_ref], targets))
    ]
    for copy in copies[:-1]:
        copy.start()
    y_ref[...] = section_output(x_ref, own_ref, arrived)
    copies[-1].start()
    for copy in copies:
        copy.wait()


def collect(x, own, arrived, earlier, spots):
    return pl.pallas_call(
        functools.partial(collect_kernel, len(arrived), spots),
        out_shape=jax.ShapeDtypeStruct((TICK_COUNT, 2, 1, *x.shape), jnp.bfloat16),
        in_specs=[IN_VMEM] * (2 + len(arrived)) + [IN_PLACE] * len(earlier),
        out_specs=IN_PLACE,
        scratch_shapes=[
            pltpu.VMEM(x.shape, jnp.bfloat16),
            pltpu.SemaphoreType.DMA((len(spots),)),
        ],
        compiler_params=pltpu.CompilerParams(vmem_limit_bytes=6 * 2**20),
        name="collect",
    )(x, own, *arrived, *earlier)


def send(values, target):
    pipe, tensor = lax.axis_size("pipe"), lax.axis_size("tensor")
    pairs = []
    for k in range(pipe):
        for z in range(tensor):
            to_k, to_z = target(k, z)
            pairs.append((k * tensor + z, to_k * tensor + to_z))
    return lax.ppermute(values, ("pipe", "tensor"), pairs)


def first_halving(partials, after):
    partials = list(partials)
    for apart in reversed(range(3, len(partials), 2)):
        incoming = send(partials[apart], lambda k, z: (k, z ^ 1))
        incoming, after = lax.optimization_barrier((incoming, after))
        partials[apart ^ 1] = partials[apart ^ 1] + incoming.astype(jnp.float32)
    kept = partials[:2] + [
        partial.astype(jnp.bfloat16) if apart == 2 else partial
        for apart, partial in enumerate(partials)
        if apart >= 2 and apart % 2 == 0
    ]
    return kept, after


def other_halvings(partials):
    pair, rest = partials[:2], partials[2:]
    arrived = []
    left = {2 * (spot + 1): partial for spot, partial in enumerate(rest)}
    bit = 2
    while left:
        for apart in sorted(left, reverse=True):
            if apart & bit:
                incoming = send(
                    left.pop(apart).astype(jnp.bfloat16), lambda k, z: (k, z ^ bit)
                )
                if apart == bit:
                    arrived.append(incoming)
                else:
                    left[apart ^ bit] = left[apart ^ bit].astype(jnp.float32) + incoming.astype(
                        jnp.float32
                    )
        bit *= 2
    return arrived + [send(pair[1], lambda k, z: (k, z ^ 1))]


def local(
    down_state, up_state, layer_proj, conv_filters, norm_gains, embedding, dna_tokens, entry_order
):
    pipe, tensor = lax.axis_size("pipe"), lax.axis_size("tensor")
    gains = norm_gains

    def mirrored(k):
        return pipe - 1 - k

    def following(k):
        return (k + 1) % pipe

    def spread(sums, target):
        return [
            send(sums, lambda k, z, apart=apart: (target(k), z ^ apart))
            for apart in range(1, tensor)
        ]

    down, up = 0, 1
    entering = [down_state[0], up_state[0]]
    sums = squares_of(*entering)
    entering[up], sums = lax.optimization_barrier((entering[up], sums))
    entering[up] = send(entering[up], lambda k, z: (mirrored(k), z))
    squares = [spread(sums, lambda k: k), spread(sums, mirrored)]
    blocks, weight, fresh = prepare(
        conv_filters[0], layer_proj[0], dna_tokens, entry_order, embedding
    )

    def go_on(partials):
        own, *rest = partials
        rest = lax.optimization_barrier(rest)
        return own, other_halvings([own, *rest]), rest[1:2]

    def run_layer(way, tick, after):
        *partials, neighbour = layer_partials(
            entering[way],
            squares[way],
            way if tick == 0 else 0,
            gains,
            blocks,
            weight,
            tensor,
            after,
        )
        if (way, tick) in ((up, 1), (down, 2)):
            neighbour, y = lax.optimization_barrier((neighbour, leaving[up].pop()))
            leaving[up].append(send(y, lambda k, z: (mirrored(k), z)))
        return [*partials, neighbour]

    def finish(way, tick, own, arrived):
        after = leaving[up][-1:] if (way, tick) in ((down, 0), (up, 2)) else []
        if tick == TICK_COUNT - 1:
            leaving[way].append(end(entering[way], own, arrived, after))
            return
        y, sent, sums = merge(entering[way], fresh[way][tick], own, arrived, after)
        leaving[way].append(y)
        entering[way] = send(sent, lambda k, z: (following(k), z))
        squares[way] = spread(sums, following)

    leaving = [[], []]
    partials, _ = first_halving(run_layer(up, 0, []), [])
    own, arrived, early = go_on(partials)
    for turn in range(1, 2 * TICK_COUNT):
        way, tick = (up, down)[turn % 2], turn // 2
        partials = run_layer(way, tick, early)
        finish(1 - way, (turn - 1) // 2, own, arrived)
        ending = turn == 2 * TICK_COUNT - 1
        held = [leaving[up].pop()] if ending else []
        partials, held = first_halving(partials, held)
        leaving[up].extend(held)
        own, arrived, early = go_on(partials)
    leaving[up].append(send(leaving[up].pop(), lambda k, z: (mirrored(k), z)))
    earlier = [*leaving[down], *leaving[up]]
    spots = [(tick, down) for tick in range(TICK_COUNT - 1)]
    spots += [(tick, up) for tick in range(TICK_COUNT)] + [(TICK_COUNT - 1, down)]
    return collect(entering[down], own, arrived, earlier, spots)


def solution(mesh):
    placed = (
        P("pipe", None, "tensor"),
        P("pipe", None, "tensor"),
        P("pipe", "tensor", None),
        P("pipe", "tensor", None),
        P("pipe", "tensor"),
        P(None, "tensor"),
        P(),
        P(),
    )
    return jax.shard_map(
        local,
        mesh=mesh,
        in_specs=placed,
        out_specs=P(None, None, "pipe", None, "tensor"),
        check_vma=False,
    )
```
